32 devices in a mesh: req: 4 (over z), head: 4 (over y, x), blk: 2 (over core).
Axes of the slice: x: 2, y: 2, z: 4, core: 2. Of those that a mesh axis runs over, the one named last changes fastest.
Arguments:
- group_rows: bfloat16 [8, 256, 2048], P(None, 'req', ('head', 'blk')), may hold values from -6 to 6
- slot_request: int32 [8], replicated, may hold values from 0 to 7, each once
- cache_len: int32 [8], replicated, may hold values from 1 to 512, as said below
- group_len: int32 [8], replicated, may hold values from 1 to 256, as said below
- attn_cache: bfloat16 [2, 8, 512, 2048], P(None, 'req', None, ('head', 'blk')), as said below
- hand_cache: bfloat16 [2, 2, 8, 512, 2048], P('blk', None, None, 'req', 'head'), may hold values from -6 to 6
- query_weight: bfloat16 [2048, 2048], P(None, ('head', 'blk')), may hold values from -0.125 to 0.125
- key_weight: bfloat16 [2048, 2048], P(None, ('head', 'blk')), may hold values from -0.125 to 0.125
- value_weight: bfloat16 [2048, 2048], P(None, ('head', 'blk')), may hold values from -0.125 to 0.125
- out_weight: bfloat16 [2048, 2048], P(('head', 'blk')), may hold values from -0.125 to 0.125
- query_gain: float32 [2048], P(('head', 'blk')), may hold values from 0.5 to 1.5
- key_gain: float32 [2048], P(('head', 'blk')), may hold values from 0.5 to 1.5
- attn_gain: float32 [2048], replicated, may hold values from 0.1 to 1.9
- mlp_gain: float32 [2048], replicated, may hold values from 0.1 to 1.9
- gate_weight: bfloat16 [2048, 4096], P(None, ('head', 'blk')), may hold values from -0.125 to 0.125
- up_weight: bfloat16 [2048, 4096], P(None, ('head', 'blk')), may hold values from -0.125 to 0.125
- down_weight: bfloat16 [4096, 2048], P(('head', 'blk')), may hold values from -0.09375 to 0.09375
Outputs:
- layer_out: bfloat16 [8, 256, 2048], P(None, 'req', ('head', 'blk'))
- relaid: bfloat16 [2, 2, 8, 512, 2048], P('blk', None, 'req', None, 'head')
The draws below stay inside these ranges and needn't reach their ends.
Inputs may be any that keep to these rules, and one draw needn't show every extreme that they name: `cache_len`: some request has exactly 512 cached tokens. `group_len`: some request has exactly 256 valid new tokens. `attn_cache`: entry s along the request dimension belongs to request slot_request[s]; positions from cache_len of that request on are not read.
All inputs are finite; a program needn't handle non-finite values.
Results may differ from the reference program's by a relative error of at most 0.009.
The reference program's roundings to bfloat16 on the way (of `ordered`, `keys_new`, `weights`, `attended`, `state`, `inner` and `result`) count: a program that leaves them out, or rounds other values in their place, can miss the bound.
Values may be sent and summed in bfloat16 or wider, within the bound.
A program may use at most 128 MiB of HBM per device.

```python
import jax
import jax.numpy as jnp
from jax import lax

D = 2048
HD = 128
FF = 4096
CTX = 512
GROUP = 256
HAND_LAYERS = 2
REQUESTS = 8


def draw_cache_len(key, part):
    values = jax.random.randint(jax.random.fold_in(key, 11), (REQUESTS,), 1, CTX + 1).astype(jnp.int32)
    where_top = jax.random.randint(jax.random.fold_in(key, 12), (), 0, REQUESTS)
    return values.at[where_top].set(CTX)


def draw_group_len(key, part):
    values = jax.random.randint(jax.random.fold_in(key, 21), (REQUESTS,), 1, GROUP + 1).astype(jnp.int32)
    where_top = jax.random.randint(jax.random.fold_in(key, 22), (), 0, REQUESTS)
    return values.at[where_top].set(GROUP)


def draw_attn_cache(key, part):
    shape = (REQUESTS, CTX, D)
    keys = jax.random.normal(jax.random.fold_in(key, 37), shape, jnp.float32)
    values = jax.random.normal(jax.random.fold_in(key, 38), shape, jnp.float32)
    return jnp.stack([keys, values], axis=0).astype(jnp.bfloat16)


def steps_of(rng, extent, shards, smallest, top_value):
    def one(dim, blocks):
        heights = jax.random.uniform(jax.random.fold_in(jax.random.fold_in(rng, 6), dim), (blocks,), jnp.float32, smallest / len(shards), top_value / len(shards))
        return jnp.repeat(jnp.exp(heights), extent[dim] // blocks).reshape((-1,) + (1,) * (len(extent) - dim - 1))

    loudness = one(*shards[0])
    for cut in shards[1:]:
        loudness = loudness * one(*cut)
    return loudness


def scatter_about(stream_key, dims, deviation, limit, pieces=(), kind=jnp.bfloat16):
    loudness = steps_of(stream_key, dims, pieces, -0.22, 0.18) if pieces else 1.0
    array = jax.random.normal(stream_key, dims, jnp.float32) * deviation * loudness
    return jnp.minimum(jnp.maximum(array, -limit), limit).astype(kind)


def setup_inputs(seed: int = 0) -> dict:
    key_list = jax.random.split(jax.random.key(seed), 18)
    group_rows = scatter_about(key_list[0], (REQUESTS, GROUP, D), 1.0, 6.0, ((1, 4), (2, 8)))
    slot_request = jax.random.permutation(key_list[1], REQUESTS).astype(jnp.int32)
    cache_len = draw_cache_len(jax.random.fold_in(key_list[17], 71), 0)
    group_len = draw_group_len(jax.random.fold_in(key_list[17], 71), 0)
    attn_cache = draw_attn_cache(jax.random.fold_in(key_list[17], 71), 0)
    hand_cache = scatter_about(key_list[5], (HAND_LAYERS, 2, REQUESTS, CTX, D), 1.0, 6.0, ((0, 2), (3, 4), (4, 4)))
    query_weight = scatter_about(key_list[6], (D, D), D ** -0.5, 0.125, ((1, 8),))
    key_weight = scatter_about(key_list[7], (D, D), D ** -0.5, 0.125, ((1, 8),))
    value_weight = scatter_about(key_list[8], (D, D), D ** -0.5, 0.125, ((1, 8),))
    out_weight = scatter_about(key_list[9], (D, D), D ** -0.5, 0.125, ((0, 8),))
    query_gain = jnp.clip(1.0 + 0.1 * jax.random.normal(key_list[10], (D,), jnp.float32), 0.5, 1.5)
    key_gain = jnp.clip(1.0 + 0.1 * jax.random.normal(key_list[11], (D,), jnp.float32), 0.5, 1.5)
    attn_gain = jnp.clip(1.0 + 0.18 * jax.random.normal(key_list[12], (D,), jnp.float32), 0.1, 1.9)
    mlp_gain = jnp.clip(1.0 + 0.18 * jax.random.normal(key_list[13], (D,), jnp.float32), 0.1, 1.9)
    gate_weight = scatter_about(key_list[14], (D, FF), D ** -0.5, 0.125, ((1, 8),))
    up_weight = scatter_about(key_list[15], (D, FF), D ** -0.5, 0.125, ((1, 8),))
    down_weight = scatter_about(key_list[16], (FF, D), FF ** -0.5, 0.09375, ((0, 8),))
    return {"group_rows": group_rows, "slot_request": slot_request, "cache_len": cache_len, "group_len": group_len, "attn_cache": attn_cache, "hand_cache": hand_cache, "query_weight": query_weight, "key_weight": key_weight, "value_weight": value_weight, "out_weight": out_weight, "query_gain": query_gain, "key_gain": key_gain, "attn_gain": attn_gain, "mlp_gain": mlp_gain, "gate_weight": gate_weight, "up_weight": up_weight, "down_weight": down_weight}


EPSILON = 1e-06
ROPE_BASE = 500000.0

def rms_scale(values, gain):
    return values * lax.rsqrt(lax.optimization_barrier(jnp.mean(values * values, axis=-1, keepdims=True)) + EPSILON) * gain

def rotate(values, places):
    half_dim = values.shape[-1] // 2
    frequency = ROPE_BASE ** (-(jnp.arange(half_dim, dtype=jnp.float32) * 2.0 / values.shape[-1]))
    angles = places[..., None].astype(jnp.float32) * frequency
    cosine_part = jnp.cos(angles)[..., None, :]
    sine_part = jnp.sin(angles)[..., None, :]
    first_half = values[..., :half_dim]
    second_half = values[..., half_dim:]
    return jnp.concatenate([first_half * cosine_part - second_half * sine_part, second_half * cosine_part + first_half * sine_part], axis=-1)

def attend(queries, keys_new, values_new, keys_old, values_old, cached, group_valid):
    score_scale = 1.0 / queries.shape[-1] ** 0.5
    span_old = keys_old.shape[1]
    tokens = queries.shape[1]
    old_scores = jnp.einsum('sthd,sjhd->shtj', queries.astype(jnp.float32), keys_old.astype(jnp.float32)) * score_scale
    new_scores = jnp.einsum('sthd,sjhd->shtj', queries.astype(jnp.float32), keys_new.astype(jnp.float32)) * score_scale
    old_mask = (jnp.arange(span_old)[None, :] < cached[:, None])[:, None, None, :]
    columns = jnp.arange(tokens)
    new_mask = (columns[None, None, :] <= columns[None, :, None]) & (columns[None, None, :] < group_valid[:, None, None])
    new_mask = new_mask[:, None, :, :]
    scores = jnp.concatenate([jnp.where(old_mask, old_scores, -1e+30), jnp.where(new_mask, new_scores, -1e+30)], axis=-1)
    row_top = lax.optimization_barrier(jnp.max(scores, axis=-1, keepdims=True))
    weights = jnp.exp(scores - row_top)
    weights = (weights / lax.optimization_barrier(jnp.sum(weights, axis=-1, keepdims=True))).astype(jnp.bfloat16)
    stacked = jnp.concatenate([values_old, values_new], axis=1)
    return jnp.einsum('shtj,sjhd->sthd', weights.astype(jnp.float32), stacked.astype(jnp.float32))

def reference(group_rows, slot_request, cache_len, group_len, attn_cache, hand_cache, query_weight, key_weight, value_weight, out_weight, query_gain, key_gain, attn_gain, mlp_gain, gate_weight, up_weight, down_weight):
    ordered = jnp.take(group_rows, slot_request, axis=0)
    cached = jnp.take(cache_len, slot_request)
    group_valid = jnp.take(group_len, slot_request)
    tokens = ordered.shape[1]
    model_width = ordered.shape[2]
    heads = model_width // HD

    def one_slot(slot_item):
        slot_rows, keys_old, values_old, count_old, count_new = slot_item
        queries = jnp.dot(slot_rows, query_weight, preferred_element_type=jnp.float32)
        keys_new = jnp.dot(slot_rows, key_weight, preferred_element_type=jnp.float32)
        values_new = jnp.dot(slot_rows, value_weight, preferred_element_type=jnp.float32)
        queries = rms_scale(queries, query_gain)
        keys_new = rms_scale(keys_new, key_gain)
        places = count_old + jnp.arange(tokens, dtype=jnp.int32)
        queries = rotate(queries.reshape(tokens, heads, HD), places).astype(jnp.bfloat16)
        keys_new = rotate(keys_new.reshape(tokens, heads, HD), places).astype(jnp.bfloat16)
        values_new = values_new.astype(jnp.bfloat16).reshape(tokens, heads, HD)
        attended = attend(queries[None], keys_new[None], values_new[None], keys_old.reshape(1, -1, heads, HD), values_old.reshape(1, -1, heads, HD), count_old[None], count_new[None])
        return attended.astype(jnp.bfloat16).reshape(tokens, model_width)
    attended = lax.map(one_slot, (ordered, attn_cache[0], attn_cache[1], cached, group_valid))
    projected = jnp.dot(attended.reshape(-1, model_width), out_weight, preferred_element_type=jnp.float32)
    state = (ordered.reshape(-1, model_width).astype(jnp.float32) + rms_scale(projected, attn_gain)).astype(jnp.bfloat16)
    gate_act = jnp.dot(state, gate_weight, preferred_element_type=jnp.float32)
    up_act = jnp.dot(state, up_weight, preferred_element_type=jnp.float32)
    inner = (jax.nn.silu(gate_act) * up_act).astype(jnp.bfloat16)
    down_sum = jnp.dot(inner, down_weight, preferred_element_type=jnp.float32)
    result = (state.astype(jnp.float32) + rms_scale(down_sum, mlp_gain)).astype(jnp.bfloat16).reshape(ordered.shape)
    layer_out = jnp.zeros_like(group_rows).at[slot_request].set(result)
    relaid = jnp.take(hand_cache, slot_request, axis=2)
    return (layer_out, relaid)
```

```python
import functools

import jax
import jax.numpy as jnp
import numpy as np
from jax import lax
from jax.experimental import pallas as pl
from jax.experimental.pallas import tpu as pltpu
from jax.sharding import PartitionSpec as P

HD = 128


EPSILON = 1e-06
ROPE_BASE = 500000.0


BF = jnp.bfloat16
F32 = jnp.float32
TILE = 128


def layer_kernel(
    dims,
    slot_ref, clen_ref, glen_ref, group_hbm, hand, freq_hbm, ac_hbm, wq, wk, wv, wo_hbm, wg, wu, wd_hbm,
    qg_hbm, kg_hbm, ag_hbm, mg_hbm,
    landed, rel,
    group, freq, qg, kg, ag, mg,
    xfull, wqkv, wo, wgu, wd, ac, qk, stat_mine, stat_all, qb, kb, vb, attended,
    xt, ht_in, ht, cos_ref, sin_ref, acc, sb1, rb1, sc1, rc1, sb2, rb2, sc2, rc2, stfull, res,
    bsend, xz_recv, h_send, h_recv, lsem, xa_send, xa_recv, st_send, st_recv,
    r1_send, r1_recv, r2_send, r2_recv, sa_send, sa_recv, d1_send, d1_recv, d2_send, d2_recv,
    f_send, f_recv,
):
    nreq, nhead, slots, sc, tokens, tb, w, rows, seg = dims
    n8 = 2 * nhead
    model = w * n8
    r = lax.axis_index("req")
    h = lax.axis_index("head")
    b = lax.axis_index("blk")
    k = h * 2 + b
    other = 1 - b
    span = ht.shape[2]

    def dev(rr, hh, bb):
        return {"req": rr, "head": hh, "blk": bb}

    def rcopy(src, dst, ssem, rsem, rr, hh, bb):
        pltpu.make_async_remote_copy(
            src_ref=src, dst_ref=dst, send_sem=ssem, recv_sem=rsem,
            device_id=dev(rr, hh, bb), device_id_type=pl.DeviceIdType.MESH,
        ).start()

    def drain(ref, sem):
        pltpu.make_async_copy(ref, ref, sem).wait()

    barrier = pltpu.get_barrier_semaphore()

    def greet(rr, hh, bb):
        pl.semaphore_signal(
            barrier, inc=1, device_id=dev(rr, hh, bb), device_id_type=pl.DeviceIdType.MESH
        )

    def greet_z(i, carry):
        greet(lax.rem(r + i, nreq), h, b)
        return carry

    lax.fori_loop(1, nreq, greet_z, 0)
    for i in range(1, n8):
        kk = lax.rem(k + i, n8)
        greet(r, kk // 2, lax.rem(kk, 2))

    n_dest = rows // seg
    n_from = max(1, tb // rows)

    def share(m, hh, bb):
        return (2 * bb + lax.rem(lax.rem(hh, 2) + m, 2)) * 2 + hh // 2

    def greet_final(i, carry):
        chunk = (r * tb) // rows + lax.rem(i // nreq, n_from)
        m = i // (nreq * n_from)
        plane = chunk // 2
        hh = lax.rem(chunk, 2) * 2 + lax.rem(lax.rem(plane, 2) + m, 2)
        greet(lax.rem(i, nreq), hh, plane // 2)
        return carry

    lax.fori_loop(0, nreq * n_from * sc, greet_final, 0)

    loads = {}

    def load(name, src, dst):
        c = pltpu.make_async_copy(src, dst, lsem.at[len(loads)])
        c.start()
        loads[name] = c

    load("group", group_hbm, group)
    load("hand", hand, ht_in)
    load("freq", freq_hbm, freq)
    load("wq", wq, wqkv.at[:, 0:w])
    load("wk", wk, wqkv.at[:, w : 2 * w])
    load("wv", wv, wqkv.at[:, 2 * w : 3 * w])
    load("qg", qg_hbm, qg)
    load("kg", kg_hbm, kg)
    load("ac", ac_hbm, ac)
    load("wo", wo_hbm, wo)
    load("ag", ag_hbm, ag)
    load("wg", wg, wgu.at[:, 0 : wg.shape[1]])
    load("wu", wu, wgu.at[:, wg.shape[1] : 2 * wg.shape[1]])
    load("wd", wd_hbm, wd)
    load("mg", mg_hbm, mg)

    loads["group"].wait()

    def order_x(i, carry):
        xt[i] = group[slot_ref[i]]
        return carry

    lax.fori_loop(0, slots, order_x, 0)
    total = (nreq - 1) + (n8 - 1) + n8 * n_dest * sc
    pl.semaphore_wait(barrier, total)

    my_tok = pl.multiple_of(r * tb, tb)

    for m in range(sc):
        def send_x(i, carry, m=m):
            rr = lax.rem(r + i, nreq)
            rcopy(
                xt.at[rr * sc + m], xfull.at[k, m, pl.ds(my_tok, tb)],
                bsend, xz_recv.at[m, r], rr, h, b,
            )
            return carry

        lax.fori_loop(1, nreq, send_x, 0)

    def gather_send(src, dst, ssem, rsem):
        for d in (3, 1, 2) if nhead == 4 else range(1, nhead):
            rcopy(src, dst, ssem, rsem, r, h ^ d, b)
        rcopy(src, dst, ssem, rsem, r, h, other)

    def forward(full, ssem, rsem, hh):
        kk = hh * 2 + b
        drain(full(kk), rsem.at[kk])
        rcopy(full(kk), full(kk), ssem, rsem.at[kk], r, h, other)

    def got(full, rsem, kk):
        drain(full(kk), rsem.at[kk])

    def x_piece(m, src, rr):
        tok = pl.multiple_of(rr * tb, tb)
        gather_send(src, xfull.at[k, m, pl.ds(tok, tb)], xa_send.at[m], xa_recv.at[m, k])

    for m in range(sc):
        x_piece(m, xt.at[r * sc + m], r)
    for m in range(sc):
        xfull[k, m, pl.ds(my_tok, tb), :] = xt[r * sc + m]

    my_pos = pl.multiple_of(r * span, span)
    loads["hand"].wait()
    step = min(span, 32)

    def order_h(i, carry):
        s = i // (span // step)
        at = pl.multiple_of(lax.rem(i, span // step) * step, step)
        for c in range(hand.shape[0]):
            ht[c, s, pl.ds(at, step), :] = ht_in[c, slot_ref[s], pl.ds(at, step), :]
        return carry

    lax.fori_loop(0, slots * (span // step), order_h, 0)


    def send_h(i, carry):
        rr = lax.rem(r + i, nreq)
        rcopy(
            ht.at[:, pl.ds(rr * sc, sc)], rel.at[:, :, pl.ds(my_pos, span)],
            h_send, h_recv, rr, h, b,
        )
        return carry

    for m in range(sc):
        def pass_on(d, carry, m=m):
            for rr in (r + d, r - d):
                @pl.when(jnp.logical_and(rr >= 0, rr < nreq))
                def _(rr=rr):
                    here = xfull.at[k, m, pl.ds(pl.multiple_of(rr * tb, tb), tb)]
                    drain(here, xz_recv.at[m, rr])
                    x_piece(m, here, rr)
            return carry

        lax.fori_loop(1, nreq, pass_on, 0)
        if m == sc - 1:
            lax.fori_loop(1, nreq, send_h, 0)
            pltpu.make_async_copy(
                ht.at[:, pl.ds(r * sc, sc)], rel.at[:, :, pl.ds(my_pos, span)], h_recv
            ).start()

    half = HD // 2
    per_slot = tokens // TILE
    loads["freq"].wait()

    def angles(i, carry):
        m = i // per_slot
        here = pl.multiple_of(lax.rem(i, per_slot) * TILE, TILE)
        start = clen_ref[slot_ref[r * sc + m]] + here
        place = lax.broadcasted_iota(jnp.int32, (TILE, HD), 0) + start
        lane = lax.broadcasted_iota(jnp.int32, (TILE, HD), 1)
        angle = place.astype(F32) * freq[...]
        cos_ref[m, pl.ds(here, TILE), :] = jnp.cos(angle)
        sine = jnp.sin(angle)
        sin_ref[m, pl.ds(here, TILE), :] = jnp.where(lane < half, -sine, sine)
        return carry

    lax.fori_loop(0, sc * per_slot, angles, 0)

    heads_here = w // HD
    score_scale = 1.0 / HD**0.5
    ctx = ac.shape[2]
    nt = (((1,), (1,)), ((), ()))
    ff = wd.shape[0]
    far = [h ^ d for d in range(1, nhead)]

    def x_of(m):
        return lambda kk: xfull.at[kk, m]

    def st_of(m):
        return lambda kk: stfull.at[m, kk]

    def x_forward(m):
        for hh in far:
            forward(x_of(m), xa_send.at[m], xa_recv.at[m], hh)

    def project(m):
        for hh in [h] + far:
            got(x_of(m), xa_recv.at[m], hh * 2 + other)
        x = jnp.concatenate([xfull[kk, m] for kk in range(n8)], axis=1)
        y = jnp.dot(x, wqkv[:, 0 : 2 * w], preferred_element_type=F32)
        qk[m] = y
        q, kn = y[:, :w], y[:, w : 2 * w]
        q2 = jnp.sum(q * q, axis=1, keepdims=True)
        k2 = jnp.sum(kn * kn, axis=1, keepdims=True)
        lanes = lax.broadcasted_iota(jnp.int32, (TILE, TILE), 1)
        for i in range(per_slot):
            cut = slice(i * TILE, (i + 1) * TILE)
            sums = jnp.where(lanes == 0, q2[cut], jnp.where(lanes == 1, k2[cut], 0.0))
            stat_mine[m, i] = sums.T[0:8, :]
        for i in range(1, n8):
            kk = lax.rem(k + i, n8)
            rcopy(
                stat_mine.at[m], stat_all.at[m, k], st_send.at[m], st_recv.at[m, k],
                r, kk // 2, lax.rem(kk, 2),
            )
        stat_all[m, k] = stat_mine[m]
        vb[m] = jnp.dot(x, wqkv[:, 2 * w : 3 * w], preferred_element_type=F32).astype(BF)

    def finish(m):
        for i in range(1, n8):
            kk = lax.rem(k + i, n8)
            drain(stat_all.at[m, kk], st_recv.at[m, kk])
        scale = lax.rsqrt(jnp.sum(stat_all[m], axis=0) / model + EPSILON)
        for i in range(per_slot):
            cut = slice(i * TILE, (i + 1) * TILE)
            sq = jnp.concatenate([scale[i], jnp.zeros((TILE - 8, TILE), F32)], axis=0).T
            cosv = cos_ref[m, cut, :]
            sinv = sin_ref[m, cut, :]
            q = qk[m, cut, 0:w] * sq[:, 0:1] * qg[...]
            kn = qk[m, cut, w : 2 * w] * sq[:, 1:2] * kg[...]
            for hh in range(heads_here):
                lane = slice(hh * HD, (hh + 1) * HD)
                qh, kh = q[:, lane], kn[:, lane]
                qb[m, cut, lane] = (qh * cosv + pltpu.roll(qh, half, 1) * sinv).astype(BF)
                kb[m, cut, lane] = (kh * cosv + pltpu.roll(kh, half, 1) * sinv).astype(BF)

    def attend(m):
        request = slot_ref[r * sc + m]
        old_ok = lax.broadcasted_iota(jnp.int32, (tokens, ctx), 1) < clen_ref[request]
        col = lax.broadcasted_iota(jnp.int32, (tokens, tokens), 1)
        row = lax.broadcasted_iota(jnp.int32, (tokens, tokens), 0)
        new_ok = jnp.logical_and(col <= row, col < glen_ref[request])
        for hh in range(heads_here):
            cut = slice(hh * HD, (hh + 1) * HD)
            q = qb[m, :, cut]
            so = lax.dot_general(q, ac[0, m, :, cut], nt, preferred_element_type=F32) * score_scale
            sn = lax.dot_general(q, kb[m, :, cut], nt, preferred_element_type=F32) * score_scale
            so = jnp.where(old_ok, so, -1e30)
            sn = jnp.where(new_ok, sn, -1e30)
            top = jnp.maximum(
                jnp.max(so, axis=1, keepdims=True), jnp.max(sn, axis=1, keepdims=True)
            )
            po, pn = jnp.exp(so - top), jnp.exp(sn - top)
            inv = 1.0 / (jnp.sum(po, axis=1, keepdims=True) + jnp.sum(pn, axis=1, keepdims=True))
            o = jnp.dot(
                (po * inv).astype(BF), ac[1, m, :, cut], preferred_element_type=F32
            ) + jnp.dot((pn * inv).astype(BF), vb[m, :, cut], preferred_element_type=F32)
            attended[m, :, cut] = o.astype(BF)

    def to_pair(m, p, sb, rb, ssem, rsem):
        for hh in range(nhead):
            sb[m, hh] = p[hh * rows : (hh + 1) * rows].astype(BF)
        for hh in far + [h]:
            rcopy(sb.at[m, hh], rb.at[m, hh], ssem.at[m], rsem.at[m, hh], r, h, other)

    def to_chips(m, rb, sc_, rc_, rsem, ssem2, rsem2):
        for hh in far[::-1]:
            drain(rb.at[m, hh], rsem.at[m, hh])
            sc_[m, hh] = (acc[m, hh] + rb[m, hh].astype(F32)).astype(BF)
            rcopy(sc_.at[m, hh], rc_.at[m, h], ssem2.at[m], rsem2.at[m, h], r, hh, b)

    def collect(m, rb, rsem, rc_, rsem2):
        drain(rb.at[m, h], rsem.at[m, h])
        value = acc[m, h] + rb[m, h].astype(F32)
        for hh in far:
            drain(rc_.at[m, hh], rsem2.at[m, hh])
            value = value + rc_[m, hh].astype(F32)
        return value

    def out_part(m, bb):
        a = jnp.concatenate(
            [
                attended[m, pl.ds(pl.multiple_of(share(m, hh, bb) * rows, rows), rows), :]
                for hh in range(nhead)
            ],
            axis=0,
        )
        return jnp.dot(a, wo[...], preferred_element_type=F32)

    def scatter_out(m):
        to_pair(m, out_part(m, other), sb1, rb1, r1_send, r1_recv)
        p = out_part(m, b)
        for hh in range(nhead):
            acc[m, hh] = p[hh * rows : (hh + 1) * rows]

    def state_of(m):
        proj = collect(m, rb1, r1_recv, rc1, r2_recv)
        at = pl.multiple_of(share(m, h, b) * rows, rows)
        x_rows = jnp.concatenate(
            [xfull[kk, m, pl.ds(at, rows), :] for kk in range(n8)], axis=1
        ).astype(F32)
        norm = lax.rsqrt(jnp.mean(proj * proj, axis=1, keepdims=True) + EPSILON)
        stfull[m, k] = (x_rows + proj * norm * ag[...]).astype(BF)
        gather_send(stfull.at[m, k], stfull.at[m, k], sa_send.at[m], sa_recv.at[m, k])

    def st_forward(m):
        for hh in far:
            forward(st_of(m), sa_send.at[m], sa_recv.at[m], hh)

    def mlp_part(m, bb):
        s = jnp.concatenate([stfull[m, 2 * hh + bb] for hh in range(nhead)], axis=0)
        gu = jnp.dot(s, wgu[...], preferred_element_type=F32)
        g, u = gu[:, :ff], gu[:, ff:]
        inner = (g * jax.nn.sigmoid(g) * u).astype(BF)
        return jnp.dot(inner, wd[...], preferred_element_type=F32)

    def mlp_own(m):
        p = mlp_part(m, b)
        for hh in range(nhead):
            acc[m, hh] = p[hh * rows : (hh + 1) * rows]

    def mlp_pair(m):
        for hh in [h] + far:
            got(st_of(m), sa_recv.at[m], hh * 2 + other)
        to_pair(m, mlp_part(m, other), sb2, rb2, d1_send, d1_recv)

    def send_home(m):
        down = collect(m, rb2, d1_recv, rc2, d2_recv)
        norm = lax.rsqrt(jnp.mean(down * down, axis=1, keepdims=True) + EPSILON)
        result = (stfull[m, k].astype(F32) + down * norm * mg[...]).astype(BF)
        for part in range(n_dest):
            for kk in range(n8):
                res[m, part * n8 + kk] = result[part * seg : (part + 1) * seg, kk * w : (kk + 1) * w]
        slot = r * sc + m
        first = share(m, h, b) * rows

        def one(i, carry):
            kk = lax.rem(k + i // n_dest, n8)
            part = lax.rem(i, n_dest)
            rr = first // tb + part
            mine = jnp.logical_and(rr == r, kk == k)
            src = res.at[m, part * n8 + kk]
            dst = landed.at[slot, pl.ds(pl.multiple_of(lax.rem(first, tb), seg), seg)]

            @pl.when(mine)
            def _():
                pltpu.make_async_copy(src, dst, f_recv).start()

            @pl.when(jnp.logical_not(mine))
            def _():
                rcopy(src, dst, f_send.at[m], f_recv, rr, kk // 2, lax.rem(kk, 2))

            return carry

        lax.fori_loop(0, n8 * n_dest, one, 0)

    for m in range(sc):
        if m == 0:
            x_forward(m)
            for name in ("wq", "wk", "wv", "qg", "kg", "ac", "wo"):
                loads[name].wait()
        project(m)
        finish(m)
        attend(m)
        scatter_out(m)
        if m + 1 < sc:
            x_forward(m + 1)
        to_chips(m, rb1, sc1, rc1, r1_recv, r2_send, r2_recv)
    for name in ("ag", "wg", "wu", "wd", "mg"):
        loads[name].wait()
    for m in range(sc):
        state_of(m)
    for m in range(sc):
        st_forward(m)
        mlp_own(m)
        mlp_pair(m)
        to_chips(m, rb2, sc2, rc2, d1_recv, d2_send, d2_recv)
    for m in range(sc):
        send_home(m)

    drain(landed, f_recv)
    drain(rel, h_recv)
    if nreq > 1:
        drain(xt.at[pl.ds(0, (nreq - 1) * sc)], bsend)
        drain(ht.at[:, pl.ds(0, (nreq - 1) * sc)], h_send)
    for m in range(sc):
        drain(xfull.at[pl.ds(0, n8 - 1), m], xa_send.at[m])
        drain(stfull.at[m, pl.ds(0, n8 - 1)], sa_send.at[m])
        drain(stat_all.at[m, pl.ds(0, n8 - 1)], st_send.at[m])
        drain(sb1.at[m], r1_send.at[m])
        drain(sb2.at[m], d1_send.at[m])
        drain(sc1.at[m, pl.ds(0, nhead - 1)], r2_send.at[m])
        drain(sc2.at[m, pl.ds(0, nhead - 1)], d2_send.at[m])

    for m in range(sc):
        first = (share(m, h, b) * rows) // tb
        own_dest = jnp.logical_and(first <= r, r < first + n_dest)

        @pl.when(own_dest)
        def _(m=m):
            drain(res.at[m, pl.ds(0, n8 * n_dest - 1)], f_send.at[m])

        @pl.when(jnp.logical_not(own_dest))
        def _(m=m):
            drain(res.at[m], f_send.at[m])


def home_kernel(slot_ref, landed, rel_in, home, rel_out, rel_mid, mid, sems):
    cuts = rel_mid.shape[2] // 2
    parts = [
        (c, s, pl.ds(half * cuts, cuts))
        for c in range(rel_mid.shape[0])
        for s in range(rel_mid.shape[1])
        for half in range(2)
    ]
    n = len(parts)
    ins = [pltpu.make_async_copy(landed, mid, sems.at[0, n])]
    ins += [
        pltpu.make_async_copy(rel_in.at[p], rel_mid.at[p], sems.at[0, i])
        for i, p in enumerate(parts)
    ]
    outs = [
        pltpu.make_async_copy(mid.at[s], home.at[slot_ref[s]], sems.at[1, n + s])
        for s in range(mid.shape[0])
    ]
    more = [
        pltpu.make_async_copy(rel_mid.at[p], rel_out.at[p], sems.at[1, i])
        for i, p in enumerate(parts)
    ]
    for c in ins:
        c.start()
    ins[0].wait()
    for c in outs:
        c.start()
    for c, z in zip(ins[1:], more):
        c.wait()
        z.start()
    for c in outs + more:
        c.wait()


def on_device(
    group_rows,
    slot_request,
    cache_len,
    group_len,
    attn_cache,
    hand_cache,
    query_weight,
    key_weight,
    value_weight,
    out_weight,
    query_gain,
    key_gain,
    attn_gain,
    mlp_gain,
    gate_weight,
    up_weight,
    down_weight,
):
    nreq = lax.axis_size("req")
    nhead = lax.axis_size("head")
    slots, tb, w = group_rows.shape
    sc = slots // nreq
    tokens = tb * nreq
    n8 = 2 * nhead
    rows = tokens // n8
    seg = min(rows, tb)
    half = HD // 2
    frequency = (ROPE_BASE ** (-(np.arange(half) * 2.0 / HD))).astype(np.float32)
    freq = jnp.asarray(np.concatenate([frequency, frequency])[None])
    hand = hand_cache[0]
    model = w * n8
    ff = gate_weight.shape[1]
    span = hand.shape[2]
    dims = (nreq, nhead, slots, sc, tokens, tb, w, rows, seg)
    dma = pltpu.SemaphoreType.DMA
    hb = pl.BlockSpec(memory_space=pl.ANY)
    sm = pl.BlockSpec(memory_space=pltpu.SMEM)
    blocks = lambda n: pltpu.VMEM((sc, n, rows, model), BF)
    landed, rel = pl.pallas_call(
        functools.partial(layer_kernel, dims),
        out_shape=(
            jax.ShapeDtypeStruct((slots, tb, w), BF),
            jax.ShapeDtypeStruct((hand.shape[0], sc, span * nreq, hand.shape[3]), BF),
        ),
        in_specs=[sm, sm, sm] + [hb] * 15,
        out_specs=(hb, hb),
        scratch_shapes=[
            pltpu.VMEM((slots, tb, w), BF),
            pltpu.VMEM((1, HD), F32),
            pltpu.VMEM((1, w), F32),
            pltpu.VMEM((1, w), F32),
            pltpu.VMEM((1, model), F32),
            pltpu.VMEM((1, model), F32),
            pltpu.VMEM((n8, sc, tokens, w), BF),
            pltpu.VMEM((model, 3 * w), BF),
            pltpu.VMEM((w, model), BF),
            pltpu.VMEM((model, 2 * ff), BF),
            pltpu.VMEM((ff, model), BF),
            pltpu.VMEM(attn_cache.shape, BF),
            pltpu.VMEM((sc, tokens, 2 * w), F32),
            pltpu.VMEM((sc, tokens // TILE, 8, TILE), F32),
            pltpu.VMEM((sc, n8, tokens // TILE, 8, TILE), F32),
            pltpu.VMEM((sc, tokens, w), BF),
            pltpu.VMEM((sc, tokens, w), BF),
            pltpu.VMEM((sc, tokens, w), BF),
            pltpu.VMEM((sc, tokens, w), BF),
            pltpu.VMEM((slots, tb, w), BF),
            pltpu.VMEM(hand.shape, BF),
            pltpu.VMEM(hand.shape, BF),
            pltpu.VMEM((sc, tokens, HD), F32),
            pltpu.VMEM((sc, tokens, HD), F32),
            pltpu.VMEM((sc, nhead, rows, model), F32),
            blocks(nhead), blocks(nhead), blocks(nhead), blocks(nhead),
            blocks(nhead), blocks(nhead), blocks(nhead), blocks(nhead),
            blocks(n8),
            pltpu.VMEM((sc, (rows // seg) * n8, seg, w), BF),
            dma, dma((sc, nreq)), dma, dma, dma((15,)), dma((sc,)), dma((sc, n8)), dma((sc,)), dma((sc, n8)),
            dma((sc,)), dma((sc, nhead)), dma((sc,)), dma((sc, nhead)), dma((sc,)), dma((sc, n8)),
            dma((sc,)), dma((sc, nhead)), dma((sc,)), dma((sc, nhead)),
            dma((sc,)), dma,
        ],
        compiler_params=pltpu.CompilerParams(
            collective_id=0, has_side_effects=True, vmem_limit_bytes=56 * 1024 * 1024
        ),
    )(
        slot_request, cache_len, group_len, group_rows, hand, freq, attn_cache, query_weight, key_weight, value_weight,
        out_weight, gate_weight, up_weight, down_weight,
        query_gain[None], key_gain[None], attn_gain[None], mlp_gain[None],
    )
    home, rel = pl.pallas_call(
        home_kernel,
        out_shape=(
            jax.ShapeDtypeStruct((slots, tb, w), BF),
            jax.ShapeDtypeStruct(rel.shape, BF),
        ),
        in_specs=[sm, hb, hb],
        out_specs=(hb, hb),
        scratch_shapes=[
            pltpu.VMEM(rel.shape, BF),
            pltpu.VMEM((slots, tb, w), BF),
            dma((2, 2 * rel.shape[0] * rel.shape[1] + slots)),
        ],
    )(slot_request, landed, rel)
    return (home, rel[None])


def solution(mesh):
    in_specs = (
        P(None, "req", ("head", "blk")),
        P(),
        P(),
        P(),
        P(None, "req", None, ("head", "blk")),
        P("blk", None, None, "req", "head"),
        P(None, ("head", "blk")),
        P(None, ("head", "blk")),
        P(None, ("head", "blk")),
        P(("head", "blk"), None),
        P(("head", "blk")),
        P(("head", "blk")),
        P(),
        P(),
        P(None, ("head", "blk")),
        P(None, ("head", "blk")),
        P(("head", "blk"), None),
    )
    out_specs = (P(None, "req", ("head", "blk")), P("blk", None, "req", None, "head"))
    return jax.shard_map(
        on_device, mesh=mesh, in_specs=in_specs, out_specs=out_specs, check_vma=False
    )
```
